512 devices in a mesh: head: 16 (over y_lo, x, core), tok: 32 (over z, y_hi).
Axes of the slice: x: 4, y: 8 (y_hi: 4, y_lo: 2; y = y_hi * 2 + y_lo), z: 8, core: 2. Of those that a mesh axis runs over, the one named last changes fastest.
Arguments:
- query_rows: bfloat16 [2, 8192, 5120], P(None, 'tok', 'head'), may hold values from -6 to 6
- key_rows: bfloat16 [2, 8192, 5120], P(None, 'tok', 'head'), may hold values from -6 to 6
- value_rows: bfloat16 [2, 8192, 5120], P(None, 'tok', 'head'), may hold values from -8 to 8
- token_rates: float32 [2, 16, 8192], P(None, 'head', 'tok'), may hold values from 0.1 to 1
- gate_weight: bfloat16 [16, 320, 320], P('head'), may hold values from -0.3125 to 0.3125
- up_weight: bfloat16 [16, 320, 320], P('head'), may hold values from -0.3125 to 0.3125
- down_weight: bfloat16 [16, 320, 320], P('head'), may hold values from -0.3125 to 0.3125
- step_size: float32 [16], P('head'), may hold values from 0.3 to 1
- branch_gains: float32 [2, 5120], replicated, may hold values from 0.1 to 1.9
Outputs:
- block_output: float32 [2, 32, 256, 5120], P(None, 'tok', 'head')
The draws below stay inside these ranges and needn't reach their ends.
All inputs are finite; a program needn't handle non-finite values.
Results may differ from the reference program's by a relative error of at most 0.018.
Values may be sent and summed in bfloat16 or wider, within the bound.
A program may use at most 64 MiB of HBM per device.

```python
import math
import jax
import jax.numpy as jnp
from jax import lax

DH = 320
NH = 16
D = 5120
SEG_DEV = 256
SEGMENTS = 2
SEG_TOKENS = 8192
WINDOW = 256
NS_STEPS = 3
N_TOK = 32


def draw_query_rows(key, part):
    shape = (SEGMENTS, SEG_TOKENS, D)
    result = jnp.clip(jax.random.normal(jax.random.fold_in(key, 11), shape, jnp.float32), -6.0, 6.0)
    return result.astype(jnp.bfloat16)


def draw_key_rows(key, part):
    shape = (SEGMENTS, SEG_TOKENS, D)
    result = jnp.clip(jax.random.normal(jax.random.fold_in(key, 13), shape, jnp.float32), -6.0, 6.0)
    return result.astype(jnp.bfloat16)


def draw_value_rows(key, part):
    shape = (SEGMENTS, SEG_TOKENS, D)
    column = jnp.arange(D)
    head_scale = 0.6 * 3.0 ** ((column // DH).astype(jnp.float32) / max(NH - 1, 1))
    noise = jax.random.normal(jax.random.fold_in(key, 17), shape, jnp.float32)
    result = jnp.clip(noise, -4.0, 4.0) * head_scale
    return result.astype(jnp.bfloat16)


def level_of(key, dims, cuts, least, high):
    loudness = 1.0
    for axis_at, shards_of in cuts:
        steps = jax.random.uniform(jax.random.fold_in(jax.random.fold_in(key, 6), axis_at), (shards_of,), jnp.float32, least / len(cuts), high / len(cuts))
        loudness = loudness * jnp.repeat(jnp.exp(steps), dims[axis_at] // shards_of).reshape((-1,) + (1,) * (len(dims) - 1 - axis_at))
    return loudness


def centred(stream_key, extent, scale, reach, split=(), held_as=jnp.bfloat16):
    entries = scale * jax.random.normal(stream_key, extent, jnp.float32)
    if split:
        entries = entries * level_of(stream_key, extent, split, -0.22, 0.18)
    return jnp.clip(entries, -reach, reach).astype(held_as)


def setup_inputs(seed: int = 0) -> dict:
    key_of = jax.random.split(jax.random.key(seed), 10)
    return {
        "query_rows": draw_query_rows(jax.random.fold_in(key_of[9], 71), 0),
        "key_rows": draw_key_rows(jax.random.fold_in(key_of[9], 71), 0),
        "value_rows": draw_value_rows(jax.random.fold_in(key_of[9], 71), 0),
        "token_rates": jnp.clip(jnp.exp(math.log(1.0) - 2.3025851 * jax.random.uniform(key_of[3], (SEGMENTS, NH, SEG_TOKENS), jnp.float32) ** level_of(key_of[3], (SEGMENTS, NH, SEG_TOKENS), ((1, 16), (2, 32)), -0.2, 0.2)), 0.1, 1.0),
        "gate_weight": centred(key_of[4], (NH, DH, DH), DH ** -0.5, 0.3125, ((0, 16),)),
        "up_weight": centred(key_of[5], (NH, DH, DH), DH ** -0.5, 0.3125, ((0, 16),)),
        "down_weight": centred(key_of[6], (NH, DH, DH), DH ** -0.5, 0.3125, ((0, 16),)),
        "step_size": jnp.clip(jnp.exp(math.log(1.0) - 1.2039728 * jax.random.uniform(key_of[7], (NH,), jnp.float32) ** level_of(key_of[7], (NH,), ((0, 16),), -0.2, 0.2)), 0.3, 1.0),
        "branch_gains": jnp.clip(1.0 + 0.18 * jax.random.normal(key_of[8], (2, D), jnp.float32), 0.1, 1.9),
    }


NEWTON_A = 3.4445
NEWTON_B = -4.775
NEWTON_C = 2.0315
NORM_EPS = 1e-06
FROB_EPS = 1e-07

def product(left, right):
    return jnp.dot(left, right, preferred_element_type=jnp.float32)

def batched(form, left, right):
    return jnp.einsum(form, left.astype(jnp.float32), right.astype(jnp.float32), precision=lax.Precision.HIGHEST)

def gradients(key_head, value_head, rate_head, weights):
    pre_gate = product(key_head, weights[0])
    pre_up = product(key_head, weights[1])
    sig_gate = jax.nn.sigmoid(pre_gate)
    swish = pre_gate * sig_gate
    hidden = (swish * pre_up).astype(jnp.bfloat16)
    target = (-(rate_head[:, None] * value_head.astype(jnp.float32))).astype(jnp.bfloat16)
    grad_down = product(hidden.T, target)
    backward = product(target, weights[2].T)
    d_gate = (backward * pre_up * sig_gate * (1.0 + pre_gate * (1.0 - sig_gate))).astype(jnp.bfloat16)
    d_up = (backward * swish).astype(jnp.bfloat16)
    return jnp.stack([product(key_head.T, d_gate), product(key_head.T, d_up), grad_down])

def orthogonalize(stacked):
    norms = jnp.sqrt(lax.optimization_barrier(jnp.sum(stacked * stacked, axis=(1, 2), keepdims=True)))
    iterate = (stacked / (norms + FROB_EPS)).astype(jnp.bfloat16)
    for sweep_index in range(NS_STEPS):
        square = batched('mij,mkj->mik', iterate, iterate).astype(jnp.bfloat16)
        mixing = (NEWTON_B * square.astype(jnp.float32) + NEWTON_C * batched('mij,mjk->mik', square, square)).astype(jnp.bfloat16)
        iterate = (NEWTON_A * iterate.astype(jnp.float32) + batched('mij,mjk->mik', mixing, iterate)).astype(jnp.bfloat16)
    return iterate

def apply_fast(query_head, weights):
    gate = product(query_head, weights[0])
    up_part = product(query_head, weights[1])
    hidden = (jax.nn.silu(gate) * up_part).astype(jnp.bfloat16)
    return product(hidden, weights[2]).astype(jnp.bfloat16)

def one_head(packed):
    query_head, key_head, value_head, rate_head, gate_head, up_head, down_head, step_head = packed
    weights = jnp.stack([gate_head, up_head, down_head])
    outputs = []
    for section_index in range(SEGMENTS):
        update = orthogonalize(gradients(key_head[section_index], value_head[section_index], rate_head[section_index], weights))
        weights = (weights.astype(jnp.float32) - step_head * update.astype(jnp.float32)).astype(jnp.bfloat16)
        outputs.append(apply_fast(query_head[section_index], weights))
    return jnp.stack(outputs)

def split_heads(array):
    return array.reshape(SEGMENTS, SEG_TOKENS, NH, DH).transpose(2, 0, 1, 3)

def window_attention(query_rows, key_rows, value_rows):
    total_rows = SEGMENTS * SEG_TOKENS
    flat_query = query_rows.reshape(total_rows, NH, DH)
    padding = jnp.zeros((WINDOW, NH, DH), jnp.bfloat16)
    flat_key = jnp.concatenate([padding, key_rows.reshape(total_rows, NH, DH)], 0)
    flat_value = jnp.concatenate([padding, value_rows.reshape(total_rows, NH, DH)], 0)
    block_rows = math.gcd(total_rows, 512)
    scale = 1.0 / math.sqrt(DH)

    def one_block(block_number):
        start = (block_number * block_rows).astype(jnp.int32)
        query_block = lax.dynamic_slice_in_dim(flat_query, start, block_rows, 0)
        key_block = lax.dynamic_slice_in_dim(flat_key, start, block_rows + WINDOW, 0)
        value_block = lax.dynamic_slice_in_dim(flat_value, start, block_rows + WINDOW, 0)
        scores = batched('qhd,khd->hqk', query_block, key_block) * scale
        query_index = jnp.arange(block_rows, dtype=jnp.int32)[:, None]
        key_index = jnp.arange(block_rows + WINDOW, dtype=jnp.int32)[None, :]
        live = (key_index > query_index) & (key_index <= query_index + WINDOW) & (start + key_index >= WINDOW)
        scores = jnp.where(live[None], scores, -1e+30)
        top = lax.optimization_barrier(jnp.max(scores, axis=-1, keepdims=True))
        expo = jnp.exp(scores - top)
        probs = (expo / lax.optimization_barrier(jnp.sum(expo, axis=-1, keepdims=True))).astype(jnp.bfloat16)
        return batched('hqk,khd->qhd', probs, value_block).astype(jnp.bfloat16)
    blocks = lax.map(one_block, jnp.arange(total_rows // block_rows, dtype=jnp.int32))
    return blocks.reshape(SEGMENTS, SEG_TOKENS, NH * DH)

def normalize(branch, gain):
    widened = branch.astype(jnp.float32)
    mean_square = lax.optimization_barrier(jnp.sum(widened * widened, axis=-1, keepdims=True)) / D
    return widened * lax.rsqrt(mean_square + NORM_EPS) * gain

def reference(query_rows, key_rows, value_rows, token_rates, gate_weight, up_weight, down_weight, step_size, branch_gains):
    packed = (split_heads(query_rows), split_heads(key_rows), split_heads(value_rows), token_rates.transpose(1, 0, 2), gate_weight, up_weight, down_weight, step_size)
    fast_heads = lax.map(one_head, packed)
    fast = fast_heads.transpose(1, 2, 0, 3).reshape(SEGMENTS, SEG_TOKENS, D)
    attended = window_attention(query_rows, key_rows, value_rows)
    combined = normalize(fast, branch_gains[0]) + normalize(attended, branch_gains[1])
    return combined.reshape(SEGMENTS, N_TOK, SEG_DEV, D)
```

```python
import functools
import math

import jax
import jax.numpy as jnp
from jax import lax
from jax.experimental import pallas as pl
from jax.experimental.pallas import tpu as pltpu
from jax.sharding import PartitionSpec as P

SEGMENTS = 2
WINDOW = 256
NS_STEPS = 3
D = 5120

NEWTON_A = 3.4445
NEWTON_B = -4.775
NEWTON_C = 2.0315
NORM_EPS = 1e-06
FROB_EPS = 1e-07

MESH = pl.DeviceIdType.MESH
BF16 = jnp.bfloat16
F32 = jnp.float32
LANES = 128
ROWS_Z = 192
ROWS_Y = 128
TILES = 8


def dot(left, right):
    return jnp.dot(left, right, preferred_element_type=F32)


def dot_tn(left, right):
    return lax.dot_general(left, right, (((0,), (0,)), ((), ())), preferred_element_type=F32)


def dot_nt(left, right):
    return lax.dot_general(left, right, (((1,), (1,)), ((), ())), preferred_element_type=F32)


def remote(src, dst, send_sem, recv_sem, where):
    return pltpu.make_async_remote_copy(
        src_ref=src,
        dst_ref=dst,
        send_sem=send_sem,
        recv_sem=recv_sem,
        device_id=where,
        device_id_type=MESH,
    )


class Exchange:
    def __init__(self, count, me, source, slot, sems, where):
        self.count, self.me = count, me
        self.source, self.slot, self.where = source, slot, where
        self.send, self.recv = sems

    def start(self):
        def step(d, _):
            peer = lax.rem(self.me + d, self.count)
            remote(
                self.source(peer),
                self.slot(self.me),
                self.send.at[d],
                self.recv.at[self.me],
                self.where(peer),
            ).start()
            return 0

        lax.fori_loop(1, self.count, step, 0)

    def wait_recv(self):
        def step(d, _):
            peer = lax.rem(self.me + d, self.count)
            remote(
                self.slot(peer), self.slot(peer), self.send.at[d], self.recv.at[peer], self.where(peer)
            ).wait_recv()
            return 0

        lax.fori_loop(1, self.count, step, 0)

    def wait_send(self):
        def step(d, _):
            peer = lax.rem(self.me + d, self.count)
            remote(
                self.source(peer),
                self.slot(self.me),
                self.send.at[d],
                self.recv.at[self.me],
                self.where(peer),
            ).wait_send()
            return 0

        lax.fori_loop(1, self.count, step, 0)


def kernel(
    nz,
    ny,
    nh,
    q_ref,
    k_ref,
    v_ref,
    rate_ref,
    gate_ref,
    up_ref,
    down_ref,
    step_ref,
    gain_ref,
    out_ref,
    za_send,
    za_recv,
    za_part,
    za_recv2,
    za_full,
    yb_send,
    yb_recv,
    yb_part,
    yb_recv2,
    yb_full,
    x_ref,
    w_ref,
    halo_k,
    halo_v,
    early_send,
    early_recv,
    late_send,
    late_recv,
    *sems,
):
    (za1, zb1, za2, zb2, za3, zb3, za4, zb4) = [(sems[2 * i], sems[2 * i + 1]) for i in range(8)]
    halo_s, halo_r, early_s, early_r, late_s, late_r = sems[16:]
    head = lax.axis_index("head")
    tok = lax.axis_index("tok")
    count = nz * ny
    z, y = tok // ny, lax.rem(tok, ny)
    after = lax.rem(tok + 1, count)
    before = lax.rem(tok + count - 1, count)
    dh = q_ref.shape[2]
    rows = q_ref.shape[1]
    own = rows // nh

    def at_z(peer):
        return {"tok": peer * ny + y}

    def at_y(peer):
        return {"tok": z * ny + peer}

    def at_head(peer):
        return {"head": peer}

    barrier = pltpu.get_barrier_semaphore()

    def greet(number, me, where):
        def step(d, _):
            pl.semaphore_signal(
                barrier, inc=1, device_id=where(lax.rem(me + d, number)), device_id_type=MESH
            )
            return 0

        lax.fori_loop(1, number, step, 0)

    greet(nz, z, at_z)
    greet(ny, y, at_y)
    greet(nh, head, at_head)
    pl.semaphore_signal(barrier, inc=1, device_id={"tok": after}, device_id_type=MESH)
    pl.semaphore_signal(barrier, inc=1, device_id={"tok": before}, device_id_type=MESH)

    def gradients(s, weights):
        keys = k_ref[s]
        pre_gate = dot(keys, weights[0])
        pre_up = dot(keys, weights[1])
        target = (-(rate_ref[s] * v_ref[s].astype(F32))).astype(BF16)
        back = dot_nt(target, weights[2])
        sig = jax.nn.sigmoid(pre_gate)
        swish = pre_gate * sig
        hidden = (swish * pre_up).astype(BF16)
        d_gate = (back * pre_up * sig * (1.0 + pre_gate * (1.0 - sig))).astype(BF16)
        d_up = (back * swish).astype(BF16)
        gg = dot_tn(keys, d_gate)
        gu = dot_tn(keys, d_up)
        gd = dot_tn(hidden, target)
        tiles = [m[:, c : c + LANES] for m in (gg, gu, gd) for c in (0, LANES)]
        tiles.append(jnp.concatenate([gg[:, 256:], gu[:, 256:]], axis=1))
        tiles.append(jnp.concatenate([gd[:, 256:], jnp.zeros_like(gd[:, 256:])], axis=1))
        lt = TILES // nz
        for i, tile in enumerate(tiles):
            for j in range(ny):
                n = ROWS_Z // ny
                za_send[s, i // lt, j, i % lt] = tile[j * n : (j + 1) * n].astype(BF16)
                n = ROWS_Y // ny
                part = tile[ROWS_Z + j * n : ROWS_Z + (j + 1) * n]
                yb_send[s, j, i // lt, i % lt] = part.astype(BF16)

    def plan(s):
        return (
            Exchange(
                nz, z, lambda p: za_send.at[s, p], lambda p: za_recv.at[s, p],
                (za1[0].at[s], za1[1].at[s]), at_z,
            ),
            Exchange(
                ny, y, lambda p: yb_send.at[s, p], lambda p: yb_recv.at[s, p],
                (zb1[0].at[s], zb1[1].at[s]), at_y,
            ),
            Exchange(
                ny, y, lambda p: za_part.at[s, p], lambda p: za_recv2.at[s, p],
                (za2[0].at[s], za2[1].at[s]), at_y,
            ),
            Exchange(
                nz, z, lambda p: yb_part.at[s, p], lambda p: yb_recv2.at[s, p],
                (zb2[0].at[s], zb2[1].at[s]), at_z,
            ),
            Exchange(
                ny, y, lambda p: za_full.at[s, z, y], lambda p: za_full.at[s, z, p],
                (za3[0].at[s], za3[1].at[s]), at_y,
            ),
            Exchange(
                nz, z, lambda p: yb_full.at[s, y, z], lambda p: yb_full.at[s, y, p],
                (zb3[0].at[s], zb3[1].at[s]), at_z,
            ),
            Exchange(
                nz, z, lambda p: za_full.at[s, z], lambda p: za_full.at[s, p],
                (za4[0].at[s], za4[1].at[s]), at_z,
            ),
            Exchange(
                ny, y, lambda p: yb_full.at[s, y], lambda p: yb_full.at[s, p],
                (zb4[0].at[s], zb4[1].at[s]), at_y,
            ),
        )

    def summed(number, me, mine, slots):
        def step(d, total):
            return total + slots(lax.rem(me + d, number)).astype(F32)

        return lax.fori_loop(1, number, step, mine.astype(F32), unroll=True)

    def sum_and_share(s, ex):
        a1, b1, a2, b2, a3, b3, a4, b4 = ex
        b1.wait_recv()
        yb_part[s] = summed(ny, y, yb_send[s, y], lambda p: yb_recv[s, p]).astype(BF16)
        b2.start()
        a1.wait_recv()
        za_part[s] = summed(nz, z, za_send[s, z], lambda p: za_recv[s, p]).astype(BF16)
        a2.start()
        b2.wait_recv()
        yb_full[s, y, z] = summed(nz, z, yb_part[s, z], lambda p: yb_recv2[s, p]).astype(BF16)
        b3.start()
        a2.wait_recv()
        za_full[s, z, y] = summed(ny, y, za_part[s, y], lambda p: za_recv2[s, p]).astype(BF16)
        a3.start()
        b3.wait_recv()
        b4.start()
        a3.wait_recv()
        a4.start()
        b4.wait_recv()
        a4.wait_recv()

    def updated(s, weights):
        lt = TILES // nz

        def tile(i):
            top = za_full[s, i // lt, :, i % lt].reshape(ROWS_Z, LANES)
            low = yb_full[s, :, i // lt, i % lt].reshape(ROWS_Y, LANES)
            return jnp.concatenate([top, low], axis=0).astype(F32)

        for m in range(3):
            for c in range(2):
                x_ref[m, :, c * LANES : (c + 1) * LANES] = tile(2 * m + c)
        tail = tile(6)
        x_ref[0, :, 256:] = tail[:, :64]
        x_ref[1, :, 256:] = tail[:, 64:]
        x_ref[2, :, 256:] = tile(7)[:, :64]
        xs = []
        for m in range(3):
            grad = x_ref[m]
            norm = jnp.sqrt(jnp.sum(jnp.sum(grad * grad, axis=1, keepdims=True), axis=0, keepdims=True))
            xs.append((grad * (1.0 / (norm + FROB_EPS))).astype(BF16))
        for _ in range(NS_STEPS):
            squares = [dot_nt(x, x).astype(BF16) for x in xs]
            mixings = [
                (NEWTON_B * sq.astype(F32) + NEWTON_C * dot(sq, sq)).astype(BF16) for sq in squares
            ]
            xs = [
                (NEWTON_A * x.astype(F32) + dot(mix, x)).astype(BF16) for mix, x in zip(mixings, xs)
            ]
        step = step_ref[0]
        return [
            (w.astype(F32) - step * x.astype(F32)).astype(BF16) for w, x in zip(weights, xs)
        ]

    def applied(s, weights):
        queries = q_ref[s]
        gate = dot(queries, weights[0])
        up = dot(queries, weights[1])
        hidden = (gate * jax.nn.sigmoid(gate) * up).astype(BF16)
        return dot(hidden, weights[2]).astype(BF16)

    def attend(s):
        first = tok == 0
        scale = 1.0 / math.sqrt(dh)
        queries = q_ref[s]
        past = dot_nt(queries, halo_k[s]) * scale
        here = dot_nt(queries, k_ref[s]) * scale
        row = lax.broadcasted_iota(jnp.int32, (rows, rows), 0)
        col = lax.broadcasted_iota(jnp.int32, (rows, rows), 1)
        limit = jnp.where(first & (s == 0), rows, 0)
        past = jnp.where(col > row + limit, past, -1e30)
        here = jnp.where(col <= row, here, -1e30)
        top = jnp.maximum(
            jnp.max(past, axis=1, keepdims=True), jnp.max(here, axis=1, keepdims=True)
        )
        past = jnp.exp(past - top)
        here = jnp.exp(here - top)
        total = jnp.sum(past, axis=1, keepdims=True) + jnp.sum(here, axis=1, keepdims=True)
        past = (past / total).astype(BF16)
        here = (here / total).astype(BF16)
        return (dot(past, halo_v[s]) + dot(here, v_ref[s])).astype(BF16)

    def halo(ref, slot, i):
        return remote(ref, slot, halo_s.at[i], halo_r.at[i], {"tok": after})

    halos = [halo(k_ref, halo_k, 0), halo(v_ref, halo_v, 1)]
    early = Exchange(
        nh, head, lambda p: early_send.at[p], lambda p: early_recv.at[p], (early_s, early_r), at_head
    )
    late = Exchange(
        nh, head, lambda p: late_send.at[p], lambda p: late_recv.at[p], (late_s, late_r), at_head
    )

    weights = [gate_ref[...], up_ref[...], down_ref[...]]
    gradients(0, weights)
    pl.semaphore_wait(barrier, (nz - 1) + (ny - 1) + (nh - 1) + 2)

    exchange = plan(0)
    exchange[0].start()
    exchange[1].start()
    for copy in halos:
        copy.start()
    sum_and_share(0, exchange)
    new = updated(0, weights)
    for i in range(3):
        w_ref[i] = new[i]
    weights = [w_ref[i] for i in range(3)]
    gradients(1, weights)
    exchange_1 = plan(1)
    exchange_1[0].start()
    exchange_1[1].start()
    for copy in halos:
        copy.wait_recv()

    @pl.when(tok == 0)
    def _():
        halo_k[1] = halo_k[0]
        halo_v[1] = halo_v[0]

    early_send[:, 0] = applied(0, weights).reshape(nh, own, dh)
    for s in range(SEGMENTS):
        early_send[:, 1 + s] = attend(s).reshape(nh, own, dh)
    early.start()
    early_recv[head] = early_send[head]
    sum_and_share(1, exchange_1)
    weights = updated(1, weights)
    late_send[...] = applied(1, weights).reshape(nh, own, dh)
    late.start()
    late_recv[head] = late_send[head]
    early.wait_recv()

    def scale_of(load):
        total = jnp.zeros((own, dh), F32)
        for p in range(nh):
            wide = load(p).astype(F32)
            total = total + wide * wide
        mean = jnp.sum(total, axis=1, keepdims=True) * (1.0 / (nh * dh))
        return lax.rsqrt(mean + NORM_EPS)

    for s in range(SEGMENTS):
        by = scale_of(lambda p: early_recv[p, 1 + s])
        for p in range(nh):
            out_ref[s, p] = early_recv[p, 1 + s].astype(F32) * by * gain_ref[1, p]
    by = scale_of(lambda p: early_recv[p, 0])
    for p in range(nh):
        out_ref[0, p] += early_recv[p, 0].astype(F32) * by * gain_ref[0, p]
    late.wait_recv()
    by = scale_of(lambda p: late_recv[p])
    for p in range(nh):
        out_ref[1, p] += late_recv[p].astype(F32) * by * gain_ref[0, p]

    for ex in (*exchange, *exchange_1, early, late):
        ex.wait_send()
    for copy in halos:
        copy.wait_send()


def on_device(
    nz,
    ny,
    query_rows,
    key_rows,
    value_rows,
    token_rates,
    gate_weight,
    up_weight,
    down_weight,
    step_size,
    branch_gains,
):
    segments, rows, dh = query_rows.shape
    nh = lax.axis_size("head")
    own = rows // nh
    lt = TILES // nz
    na, nb = ROWS_Z // ny, ROWS_Y // ny
    vmem = pl.BlockSpec(memory_space=pltpu.VMEM)
    S = segments

    def buf(*shape, dtype=BF16):
        return pltpu.VMEM(shape, dtype)

    def pair(*shape):
        return [pltpu.SemaphoreType.DMA(shape), pltpu.SemaphoreType.DMA(shape)]

    out = pl.pallas_call(
        functools.partial(kernel, nz, ny, nh),
        out_shape=jax.ShapeDtypeStruct((segments, nh, own, dh), F32),
        in_specs=[vmem] * 7 + [pl.BlockSpec(memory_space=pltpu.SMEM), vmem],
        out_specs=vmem,
        scratch_shapes=[
            buf(S, nz, ny, lt, na, LANES),
            buf(S, nz, ny, lt, na, LANES),
            buf(S, ny, lt, na, LANES),
            buf(S, ny, lt, na, LANES),
            buf(S, nz, ny, lt, na, LANES),
            buf(S, ny, nz, lt, nb, LANES),
            buf(S, ny, nz, lt, nb, LANES),
            buf(S, nz, lt, nb, LANES),
            buf(S, nz, lt, nb, LANES),
            buf(S, ny, nz, lt, nb, LANES),
            buf(3, dh, dh, dtype=F32),
            buf(3, dh, dh),
            buf(S, rows, dh),
            buf(S, rows, dh),
            buf(nh, 3, own, dh),
            buf(nh, 3, own, dh),
            buf(nh, own, dh),
            buf(nh, own, dh),
            *pair(S, nz),
            *pair(S, ny),
            *pair(S, ny),
            *pair(S, nz),
            *pair(S, ny),
            *pair(S, nz),
            *pair(S, nz),
            *pair(S, ny),
            *pair(2),
            *pair(nh),
            *pair(nh),
        ],
        compiler_params=pltpu.CompilerParams(
            collective_id=0, has_side_effects=True, vmem_limit_bytes=48 * 1024 * 1024
        ),
    )(
        query_rows,
        key_rows,
        value_rows,
        token_rates.reshape(segments, rows, 1),
        gate_weight[0],
        up_weight[0],
        down_weight[0],
        step_size,
        branch_gains.reshape(2, nh, 1, dh),
    )
    return out.transpose(0, 2, 1, 3).reshape(segments, 1, own, nh * dh)


def solution(mesh):
    tok = mesh.shape["tok"]
    ny = 4 if tok >= 32 else 2
    placed = (
        P(None, "tok", "head"),
        P(None, "tok", "head"),
        P(None, "tok", "head"),
        P(None, "head", "tok"),
        P("head", None, None),
        P("head", None, None),
        P("head", None, None),
        P("head"),
        P(),
    )
    return jax.shard_map(
        functools.partial(on_device, tok // ny, ny),
        mesh=mesh,
        in_specs=placed,
        out_specs=P(None, "tok", "head", None),
        check_vma=False,
    )
```

```python
import functools
import math

import jax
import jax.numpy as jnp
from jax import lax
from jax.experimental import pallas as pl
from jax.experimental.pallas import tpu as pltpu
from jax.sharding import PartitionSpec as P

SEGMENTS = 2
WINDOW = 256
NS_STEPS = 3
D = 5120

NEWTON_A = 3.4445
NEWTON_B = -4.775
NEWTON_C = 2.0315
NORM_EPS = 1e-06
FROB_EPS = 1e-07

MESH = pl.DeviceIdType.MESH
BF16 = jnp.bfloat16
F32 = jnp.float32
LANES = 128
ROWS_Z = 160
ROWS_Y = 160
TILES = 8
PIECES = 4
HALO_AT = (2, 2, 2, 2, 5, 3)


def dot(left, right):
    return jnp.dot(left, right, preferred_element_type=F32)


def dot_tn(left, right):
    return lax.dot_general(left, right, (((0,), (0,)), ((), ())), preferred_element_type=F32)


def dot_nt(left, right):
    return lax.dot_general(left, right, (((1,), (1,)), ((), ())), preferred_element_type=F32)


def remote(src, dst, send_sem, recv_sem, where):
    return pltpu.make_async_remote_copy(
        src_ref=src,
        dst_ref=dst,
        send_sem=send_sem,
        recv_sem=recv_sem,
        device_id=where,
        device_id_type=MESH,
    )


class Exchange:
    def __init__(self, count, me, source, slot, sems, where):
        self.count, self.me = count, me
        self.source, self.slot, self.where = source, slot, where
        self.send, self.recv = sems

    def start(self):
        def step(d, _):
            peer = lax.rem(self.me + d, self.count)
            remote(
                self.source(peer),
                self.slot(self.me),
                self.send.at[d],
                self.recv.at[self.me],
                self.where(peer),
            ).start()
            return 0

        lax.fori_loop(1, self.count, step, 0)

    def wait_recv(self):
        def step(d, _):
            peer = lax.rem(self.me + d, self.count)
            remote(
                self.slot(peer), self.slot(peer), self.send.at[d], self.recv.at[peer], self.where(peer)
            ).wait_recv()
            return 0

        lax.fori_loop(1, self.count, step, 0)

    def wait_send(self):
        def step(d, _):
            peer = lax.rem(self.me + d, self.count)
            remote(
                self.source(peer),
                self.slot(self.me),
                self.send.at[d],
                self.recv.at[self.me],
                self.where(peer),
            ).wait_send()
            return 0

        lax.fori_loop(1, self.count, step, 0)


def kernel(
    nz,
    ny,
    nh,
    q_ref,
    k_ref,
    v_ref,
    rate_ref,
    gate_ref,
    up_ref,
    down_ref,
    step_ref,
    gain_ref,
    out_ref,
    za_send,
    za_recv,
    za_part,
    za_recv2,
    za_full,
    yb_send,
    yb_recv,
    yb_part,
    yb_recv2,
    yb_full,
    x_ref,
    w_ref,
    halo_ref,
    queries_ref,
    keys_ref,
    values_ref,
    fast_send,
    fast_recv,
    near_send,
    near_recv,
    late_send,
    late_recv,
    *sems,
):
    (za1, zb1, za2, zb2, za3, zb3, za4, zb4) = [(sems[2 * i], sems[2 * i + 1]) for i in range(8)]
    halo_s, halo_r, fast_s, fast_r, near_s, near_r, late_s, late_r, load_s = sems[16:]
    head = lax.axis_index("head")
    tok = lax.axis_index("tok")
    count = nz * ny
    z, y = tok // ny, lax.rem(tok, ny)
    after = lax.rem(tok + 1, count)
    before = lax.rem(tok + count - 1, count)
    dh = q_ref.shape[1]
    rows = q_ref.shape[2]
    own = rows // nh

    def at_z(peer):
        return {"tok": peer * ny + y}

    def at_y(peer):
        return {"tok": z * ny + peer}

    def at_head(peer):
        return {"head": peer}

    barrier = pltpu.get_barrier_semaphore()

    def greet(number, me, where):
        def step(d, _):
            pl.semaphore_signal(
                barrier, inc=1, device_id=where(lax.rem(me + d, number)), device_id_type=MESH
            )
            return 0

        lax.fori_loop(1, number, step, 0)

    greet(nz, z, at_z)
    greet(ny, y, at_y)
    greet(nh, head, at_head)
    pl.semaphore_signal(barrier, inc=1, device_id={"tok": after}, device_id_type=MESH)
    pl.semaphore_signal(barrier, inc=1, device_id={"tok": before}, device_id_type=MESH)

    def gradients(s, weights):
        keys = keys_ref[s]
        pre_gate = dot_tn(weights[0], keys)
        pre_up = dot_tn(weights[1], keys)
        target = (-(rate_ref[s] * values_ref[s].astype(F32))).astype(BF16)
        back = dot(weights[2], target)
        sig = jax.nn.sigmoid(pre_gate)
        swish = pre_gate * sig
        hidden = (swish * pre_up).astype(BF16)
        d_gate = (back * pre_up * sig * (1.0 + pre_gate * (1.0 - sig))).astype(BF16)
        d_up = (back * swish).astype(BF16)
        gg = dot_nt(keys, d_gate)
        gu = dot_nt(keys, d_up)
        gd = dot_nt(hidden, target)
        tiles = [m[:, c : c + LANES] for m in (gg, gu, gd) for c in (0, LANES)]
        tiles.append(jnp.concatenate([gg[:, 256:], gu[:, 256:]], axis=1))
        tiles.append(jnp.concatenate([gd[:, 256:], jnp.zeros_like(gd[:, 256:])], axis=1))
        lt = TILES // nz
        for i, tile in enumerate(tiles):
            for j in range(ny):
                n = ROWS_Z // ny
                za_send[s, i // lt, j, i % lt] = tile[j * n : (j + 1) * n].astype(BF16)
                n = ROWS_Y // ny
                part = tile[ROWS_Z + j * n : ROWS_Z + (j + 1) * n]
                yb_send[s, j, i // lt, i % lt] = part.astype(BF16)

    def plan(s):
        return (
            Exchange(
                nz, z, lambda p: za_send.at[s, p], lambda p: za_recv.at[s, p],
                (za1[0].at[s], za1[1].at[s]), at_z,
            ),
            Exchange(
                ny, y, lambda p: yb_send.at[s, p], lambda p: yb_recv.at[s, p],
                (zb1[0].at[s], zb1[1].at[s]), at_y,
            ),
            Exchange(
                ny, y, lambda p: za_part.at[s, p], lambda p: za_recv2.at[s, p],
                (za2[0].at[s], za2[1].at[s]), at_y,
            ),
            Exchange(
                nz, z, lambda p: yb_part.at[s, p], lambda p: yb_recv2.at[s, p],
                (zb2[0].at[s], zb2[1].at[s]), at_z,
            ),
            Exchange(
                ny, y, lambda p: za_full.at[s, z, y], lambda p: za_full.at[s, z, p],
                (za3[0].at[s], za3[1].at[s]), at_y,
            ),
            Exchange(
                nz, z, lambda p: yb_full.at[s, y, z], lambda p: yb_full.at[s, y, p],
                (zb3[0].at[s], zb3[1].at[s]), at_z,
            ),
            Exchange(
                nz, z, lambda p: za_full.at[s, z], lambda p: za_full.at[s, p],
                (za4[0].at[s], za4[1].at[s]), at_z,
            ),
            Exchange(
                ny, y, lambda p: yb_full.at[s, y], lambda p: yb_full.at[s, p],
                (zb4[0].at[s], zb4[1].at[s]), at_y,
            ),
        )

    def summed(number, me, mine, slots):
        def step(d, total):
            return total + slots(lax.rem(me + d, number)).astype(F32)

        return lax.fori_loop(1, number, step, mine.astype(F32), unroll=True)

    def sum_and_share(s, ex, fillers):
        a1, b1, a2, b2, a3, b3, a4, b4 = ex
        b1.start()
        a1.start()
        fillers[0]()
        b1.wait_recv()
        yb_part[s] = summed(ny, y, yb_send[s, y], lambda p: yb_recv[s, p]).astype(BF16)
        b2.start()
        a1.wait_recv()
        za_part[s] = summed(nz, z, za_send[s, z], lambda p: za_recv[s, p]).astype(BF16)
        a2.start()
        fillers[1]()
        b2.wait_recv()
        yb_full[s, y, z] = summed(nz, z, yb_part[s, z], lambda p: yb_recv2[s, p]).astype(BF16)
        b3.start()
        a2.wait_recv()
        za_full[s, z, y] = summed(ny, y, za_part[s, y], lambda p: za_recv2[s, p]).astype(BF16)
        a3.start()
        fillers[2]()
        b3.wait_recv()
        b4.start()
        a3.wait_recv()
        a4.start()
        fillers[3]()
        b4.wait_recv()
        a4.wait_recv()

    def updated(s, weights):
        lt = TILES // nz

        def tile(i):
            top = za_full[s, i // lt, :, i % lt].reshape(ROWS_Z, LANES)
            low = yb_full[s, :, i // lt, i % lt].reshape(ROWS_Y, LANES)
            return jnp.concatenate([top, low], axis=0).astype(F32)

        for m in range(3):
            for c in range(2):
                x_ref[m, :, c * LANES : (c + 1) * LANES] = tile(2 * m + c)
        tail = tile(6)
        x_ref[0, :, 256:] = tail[:, :64]
        x_ref[1, :, 256:] = tail[:, 64:]
        x_ref[2, :, 256:] = tile(7)[:, :64]
        xs = []
        for m in range(3):
            grad = x_ref[m]
            norm = jnp.sqrt(jnp.sum(jnp.sum(grad * grad, axis=1, keepdims=True), axis=0, keepdims=True))
            xs.append((grad * (1.0 / (norm + FROB_EPS))).astype(BF16))
        for _ in range(NS_STEPS):
            squares = [dot_nt(x, x).astype(BF16) for x in xs]
            mixings = [
                (NEWTON_B * sq.astype(F32) + NEWTON_C * dot(sq, sq)).astype(BF16) for sq in squares
            ]
            xs = [
                (NEWTON_A * x.astype(F32) + dot(mix, x)).astype(BF16) for mix, x in zip(mixings, xs)
            ]
        step = step_ref[0]
        return [
            (w.astype(F32) - step * x.astype(F32)).astype(BF16) for w, x in zip(weights, xs)
        ]

    def applied(s, weights):
        queries = queries_ref[s]
        gate = dot_tn(weights[0], queries)
        up = dot_tn(weights[1], queries)
        hidden = (gate * jax.nn.sigmoid(gate) * up).astype(BF16)
        return dot_tn(hidden, weights[2]).astype(BF16)

    def attend(s):
        first = tok == 0
        scale = 1.0 / math.sqrt(dh)
        queries = queries_ref[s]
        past = dot_tn(queries, halo_ref[s, 0]) * scale
        here = dot_tn(queries, keys_ref[s]) * scale
        row = lax.broadcasted_iota(jnp.int32, (rows, rows), 0)
        col = lax.broadcasted_iota(jnp.int32, (rows, rows), 1)
        limit = jnp.where(first & (s == 0), rows, 0)
        past = jnp.where(col > row + limit, past, -1e30)
        here = jnp.where(col <= row, here, -1e30)
        top = jnp.maximum(
            jnp.max(past, axis=1, keepdims=True), jnp.max(here, axis=1, keepdims=True)
        )
        past = jnp.exp(past - top)
        here = jnp.exp(here - top)
        total = jnp.sum(past, axis=1, keepdims=True) + jnp.sum(here, axis=1, keepdims=True)
        past = (past / total).astype(BF16)
        here = (here / total).astype(BF16)
        return (dot_nt(past, halo_ref[s, 1]) + dot_nt(here, values_ref[s])).astype(BF16)

    piece = dh // PIECES

    def halo(i):
        seg, which, part = i // (2 * PIECES), i // PIECES % 2, pl.ds(i % PIECES * piece, piece)
        ref = (keys_ref, values_ref)[which]
        return remote(
            ref.at[seg, part],
            halo_ref.at[seg, which, part],
            halo_s.at[i],
            halo_r.at[i],
            {"tok": after},
        )

    halos = [halo(i) for i in range(SEGMENTS * 2 * PIECES)]
    halo_at = [0]

    def send_halo(number):
        for copy in halos[halo_at[0] : halo_at[0] + number]:
            copy.start()
        halo_at[0] += number

    def to_heads(send, recv, sems):
        return Exchange(nh, head, lambda p: send.at[p], lambda p: recv.at[p], sems, at_head)

    share_fast = to_heads(fast_send, fast_recv, (fast_s, fast_r))
    share_near = to_heads(near_send, near_recv, (near_s, near_r))
    share_late = to_heads(late_send, late_recv, (late_s, late_r))

    def load(i, src, dst):
        return pltpu.make_async_copy(src, dst, load_s.at[i])

    loads = [
        load(0, k_ref.at[0], keys_ref.at[0]),
        load(1, gate_ref, w_ref.at[0]),
        load(2, up_ref, w_ref.at[1]),
        load(3, v_ref.at[0], values_ref.at[0]),
        load(4, down_ref, w_ref.at[2]),
        load(5, k_ref.at[1], keys_ref.at[1]),
        load(6, v_ref.at[1], values_ref.at[1]),
        load(7, q_ref, queries_ref),
    ]
    for copy in loads:
        copy.start()
    for copy in loads[:5]:
        copy.wait()
    weights = [w_ref[i] for i in range(3)]
    gradients(0, weights)
    for copy in loads[5:]:
        copy.wait()
    pl.semaphore_wait(barrier, (nz - 1) + (ny - 1) + (nh - 1) + 2)

    exchange = plan(0)
    sum_and_share(0, exchange, [lambda n=n: send_halo(n) for n in HALO_AT[:4]])
    send_halo(HALO_AT[4])
    new = updated(0, weights)
    for i in range(3):
        w_ref[i] = new[i]
    weights = [w_ref[i] for i in range(3)]
    gradients(1, weights)
    exchange_1 = plan(1)

    def fill_0():
        send_halo(HALO_AT[5])
        fast_send[...] = applied(0, weights).reshape(nh, own, dh)
        share_fast.start()
        fast_recv[head] = fast_send[head]

    def fill_3():
        for copy in halos:
            copy.wait_recv()

        @pl.when(tok == 0)
        def _():
            halo_ref[1] = halo_ref[0]

        for s in range(SEGMENTS):
            near_send[:, s] = attend(s).reshape(nh, own, dh)
        share_near.start()
        near_recv[head] = near_send[head]

    sum_and_share(1, exchange_1, [fill_0, lambda: None, lambda: None, fill_3])
    weights = updated(1, weights)
    late_send[...] = applied(1, weights).reshape(nh, own, dh)
    share_late.start()
    late_recv[head] = late_send[head]

    def scale_of(load):
        total = jnp.zeros((own, dh), F32)
        for p in range(nh):
            wide = load(p).astype(F32)
            total = total + wide * wide
        mean = jnp.sum(total, axis=1, keepdims=True) * (1.0 / (nh * dh))
        return lax.rsqrt(mean + NORM_EPS)

    def scaled(load, gain):
        by = scale_of(load)
        for p in range(0, nh, 2):
            both = jnp.concatenate([load(p), load(p + 1)], axis=1).astype(F32)
            part = slice(p * dh, (p + 2) * dh)
            yield part, both * by * gain_ref[gain : gain + 1, part]

    share_fast.wait_recv()
    for part, value in scaled(lambda p: fast_recv[p], 0):
        out_ref[0, 0, :, part] = value
    share_near.wait_recv()
    for part, value in scaled(lambda p: near_recv[p, 0], 1):
        out_ref[0, 0, :, part] += value
    for part, value in scaled(lambda p: near_recv[p, 1], 1):
        out_ref[1, 0, :, part] = value
    share_late.wait_recv()
    for part, value in scaled(lambda p: late_recv[p], 0):
        out_ref[1, 0, :, part] += value

    for ex in (*exchange, *exchange_1, share_fast, share_near, share_late):
        ex.wait_send()
    for copy in halos:
        copy.wait_send()


def on_device(
    nz,
    ny,
    query_rows,
    key_rows,
    value_rows,
    token_rates,
    gate_weight,
    up_weight,
    down_weight,
    step_size,
    branch_gains,
):
    segments, rows, dh = query_rows.shape
    nh = lax.axis_size("head")
    own = rows // nh
    lt = TILES // nz
    na, nb = ROWS_Z // ny, ROWS_Y // ny
    vmem = pl.BlockSpec(memory_space=pltpu.VMEM)
    hbm = pl.BlockSpec(memory_space=pltpu.HBM)
    S = segments

    def buf(*shape, dtype=BF16):
        return pltpu.VMEM(shape, dtype)

    def pair(*shape):
        return [pltpu.SemaphoreType.DMA(shape), pltpu.SemaphoreType.DMA(shape)]

    return pl.pallas_call(
        functools.partial(kernel, nz, ny, nh),
        out_shape=jax.ShapeDtypeStruct((segments, 1, own, nh * dh), F32),
        in_specs=[hbm] * 3 + [vmem] + [hbm] * 3 + [pl.BlockSpec(memory_space=pltpu.SMEM), vmem],
        out_specs=vmem,
        scratch_shapes=[
            buf(S, nz, ny, lt, na, LANES),
            buf(S, nz, ny, lt, na, LANES),
            buf(S, ny, lt, na, LANES),
            buf(S, ny, lt, na, LANES),
            buf(S, nz, ny, lt, na, LANES),
            buf(S, ny, nz, lt, nb, LANES),
            buf(S, ny, nz, lt, nb, LANES),
            buf(S, nz, lt, nb, LANES),
            buf(S, nz, lt, nb, LANES),
            buf(S, ny, nz, lt, nb, LANES),
            buf(3, dh, dh, dtype=F32),
            buf(3, dh, dh),
            buf(S, 2, dh, rows),
            buf(S, dh, rows),
            buf(S, dh, rows),
            buf(S, dh, rows),
            buf(nh, own, dh),
            buf(nh, own, dh),
            buf(nh, S, own, dh),
            buf(nh, S, own, dh),
            buf(nh, own, dh),
            buf(nh, own, dh),
            *pair(S, nz),
            *pair(S, ny),
            *pair(S, ny),
            *pair(S, nz),
            *pair(S, ny),
            *pair(S, nz),
            *pair(S, nz),
            *pair(S, ny),
            *pair(S * 2 * PIECES),
            *pair(nh),
            *pair(nh),
            *pair(nh),
            pltpu.SemaphoreType.DMA((8,)),
        ],
        compiler_params=pltpu.CompilerParams(
            collective_id=0, has_side_effects=True, vmem_limit_bytes=48 * 1024 * 1024
        ),
    )(
        query_rows.swapaxes(1, 2),
        key_rows.swapaxes(1, 2),
        value_rows.swapaxes(1, 2),
        token_rates,
        gate_weight[0],
        up_weight[0],
        down_weight[0],
        step_size,
        branch_gains,
    )


def solution(mesh):
    tok = mesh.shape["tok"]
    ny = 4 if tok >= 32 else 2
    placed = (
        P(None, "tok", "head"),
        P(None, "tok", "head"),
        P(None, "tok", "head"),
        P(None, "head", "tok"),
        P("head", None, None),
        P("head", None, None),
        P("head", None, None),
        P("head"),
        P(),
    )
    return jax.shard_map(
        functools.partial(on_device, tok // ny, ny),
        mesh=mesh,
        in_specs=placed,
        out_specs=P(None, "tok", "head", None),
        check_vma=False,
    )
```

```python
import functools
import math

import jax
import jax.numpy as jnp
from jax import lax
from jax.experimental import pallas as pl
from jax.experimental.pallas import tpu as pltpu
from jax.sharding import PartitionSpec as P

SEGMENTS = 2
WINDOW = 256
NS_STEPS = 3
D = 5120

NEWTON_A = 3.4445
NEWTON_B = -4.775
NEWTON_C = 2.0315
NORM_EPS = 1e-06
FROB_EPS = 1e-07

MESH = pl.DeviceIdType.MESH
BF16 = jnp.bfloat16
F32 = jnp.float32
LANES = 128
ROWS_Z = 160
ROWS_Y = 160
TILES = 8
PIECES = 4
HALO_AT = (2, 2, 2, 2, 5, 3)


def dot(left, right):
    return jnp.dot(left, right, preferred_element_type=F32)


def dot_tn(left, right):
    return lax.dot_general(left, right, (((0,), (0,)), ((), ())), preferred_element_type=F32)


def dot_nt(left, right):
    return lax.dot_general(left, right, (((1,), (1,)), ((), ())), preferred_element_type=F32)


def remote(src, dst, send_sem, recv_sem, where):
    return pltpu.make_async_remote_copy(
        src_ref=src,
        dst_ref=dst,
        send_sem=send_sem,
        recv_sem=recv_sem,
        device_id=where,
        device_id_type=MESH,
    )


class Exchange:
    def __init__(self, count, me, source, slot, sems, where):
        self.count, self.me = count, me
        self.source, self.slot, self.where = source, slot, where
        self.send, self.recv = sems

    def start(self):
        def step(d, _):
            peer = lax.rem(self.me + d, self.count)
            remote(
                self.source(peer),
                self.slot(self.me),
                self.send.at[d],
                self.recv.at[self.me],
                self.where(peer),
            ).start()
            return 0

        lax.fori_loop(1, self.count, step, 0)

    def wait_recv(self):
        def step(d, _):
            peer = lax.rem(self.me + d, self.count)
            remote(
                self.slot(peer), self.slot(peer), self.send.at[d], self.recv.at[peer], self.where(peer)
            ).wait_recv()
            return 0

        lax.fori_loop(1, self.count, step, 0)

    def wait_send(self):
        def step(d, _):
            peer = lax.rem(self.me + d, self.count)
            remote(
                self.source(peer),
                self.slot(self.me),
                self.send.at[d],
                self.recv.at[self.me],
                self.where(peer),
            ).wait_send()
            return 0

        lax.fori_loop(1, self.count, step, 0)


def kernel(
    nz,
    ny,
    nh,
    q_ref,
    k_ref,
    v_ref,
    rate_ref,
    gate_ref,
    up_ref,
    down_ref,
    step_ref,
    gain_ref,
    out_ref,
    za_send,
    za_recv,
    za_part,
    za_recv2,
    za_full,
    yb_send,
    yb_recv,
    yb_part,
    yb_recv2,
    yb_full,
    w_ref,
    halo_ref,
    queries_ref,
    keys_ref,
    values_ref,
    fast_send,
    fast_recv,
    near_send,
    near_recv,
    late_send,
    late_recv,
    *sems,
):
    (za1, zb1, za2, zb2, za3, zb3, za4, zb4) = [(sems[2 * i], sems[2 * i + 1]) for i in range(8)]
    halo_s, halo_r, fast_s, fast_r, near_s, near_r, late_s, late_r, load_s = sems[16:]
    head = lax.axis_index("head")
    tok = lax.axis_index("tok")
    count = nz * ny
    z, y = tok // ny, lax.rem(tok, ny)
    after = lax.rem(tok + 1, count)
    before = lax.rem(tok + count - 1, count)
    dh = q_ref.shape[1]
    rows = q_ref.shape[2]
    own = rows // nh

    def at_z(peer):
        return {"tok": peer * ny + y}

    def at_y(peer):
        return {"tok": z * ny + peer}

    def at_head(peer):
        return {"head": peer}

    barrier = pltpu.get_barrier_semaphore()

    def greet(number, me, where):
        def step(d, _):
            pl.semaphore_signal(
                barrier, inc=1, device_id=where(lax.rem(me + d, number)), device_id_type=MESH
            )
            return 0

        lax.fori_loop(1, number, step, 0)

    greet(nz, z, at_z)
    greet(ny, y, at_y)
    greet(nh, head, at_head)
    pl.semaphore_signal(barrier, inc=1, device_id={"tok": after}, device_id_type=MESH)
    pl.semaphore_signal(barrier, inc=1, device_id={"tok": before}, device_id_type=MESH)

    def gradients(s, weights):
        keys = keys_ref[s]
        pre_gate = dot_tn(weights[0], keys)
        pre_up = dot_tn(weights[1], keys)
        target = (-(rate_ref[s] * values_ref[s].astype(F32))).astype(BF16)
        back = dot(weights[2], target)
        sig = jax.nn.sigmoid(pre_gate)
        swish = pre_gate * sig
        hidden = (swish * pre_up).astype(BF16)
        d_gate = (back * pre_up * sig * (1.0 + pre_gate * (1.0 - sig))).astype(BF16)
        d_up = (back * swish).astype(BF16)
        gg = dot_nt(keys, d_gate)
        gu = dot_nt(keys, d_up)
        gd = dot_nt(hidden, target)
        tiles = [m[:, c : c + LANES] for m in (gg, gu, gd) for c in (0, LANES)]
        tiles.append(jnp.concatenate([gg[:, 256:], gu[:, 256:]], axis=1))
        tiles.append(jnp.concatenate([gd[:, 256:], jnp.zeros_like(gd[:, 256:])], axis=1))
        lt = TILES // nz
        for i, tile in enumerate(tiles):
            for j in range(ny):
                n = ROWS_Z // ny
                za_send[s, i // lt, j, i % lt] = tile[j * n : (j + 1) * n].astype(BF16)
                n = ROWS_Y // ny
                part = tile[ROWS_Z + j * n : ROWS_Z + (j + 1) * n]
                yb_send[s, j, i // lt, i % lt] = part.astype(BF16)

    def plan(s):
        return (
            Exchange(
                nz, z, lambda p: za_send.at[s, p], lambda p: za_recv.at[s, p],
                (za1[0].at[s], za1[1].at[s]), at_z,
            ),
            Exchange(
                ny, y, lambda p: yb_send.at[s, p], lambda p: yb_recv.at[s, p],
                (zb1[0].at[s], zb1[1].at[s]), at_y,
            ),
            Exchange(
                ny, y, lambda p: za_part.at[s, p], lambda p: za_recv2.at[s, p],
                (za2[0].at[s], za2[1].at[s]), at_y,
            ),
            Exchange(
                nz, z, lambda p: yb_part.at[s, p], lambda p: yb_recv2.at[s, p],
                (zb2[0].at[s], zb2[1].at[s]), at_z,
            ),
            Exchange(
                ny, y, lambda p: za_full.at[s, z, y], lambda p: za_full.at[s, z, p],
                (za3[0].at[s], za3[1].at[s]), at_y,
            ),
            Exchange(
                nz, z, lambda p: yb_full.at[s, y, z], lambda p: yb_full.at[s, y, p],
                (zb3[0].at[s], zb3[1].at[s]), at_z,
            ),
            Exchange(
                nz, z, lambda p: za_full.at[s, z], lambda p: za_full.at[s, p],
                (za4[0].at[s], za4[1].at[s]), at_z,
            ),
            Exchange(
                ny, y, lambda p: yb_full.at[s, y], lambda p: yb_full.at[s, p],
                (zb4[0].at[s], zb4[1].at[s]), at_y,
            ),
        )

    def summed(number, me, mine, slots):
        def step(d, total):
            return total + slots(lax.rem(me + d, number)).astype(F32)

        return lax.fori_loop(1, number, step, mine.astype(F32), unroll=True)

    def sum_and_share(s, ex, fillers):
        a1, b1, a2, b2, a3, b3, a4, b4 = ex
        b1.start()
        a1.start()
        fillers[0]()
        b1.wait_recv()
        yb_part[s] = summed(ny, y, yb_send[s, y], lambda p: yb_recv[s, p]).astype(BF16)
        b2.start()
        a1.wait_recv()
        za_part[s] = summed(nz, z, za_send[s, z], lambda p: za_recv[s, p]).astype(BF16)
        a2.start()
        fillers[1]()
        b2.wait_recv()
        yb_full[s, y, z] = summed(nz, z, yb_part[s, z], lambda p: yb_recv2[s, p]).astype(BF16)
        b3.start()
        a2.wait_recv()
        za_full[s, z, y] = summed(ny, y, za_part[s, y], lambda p: za_recv2[s, p]).astype(BF16)
        a3.start()
        fillers[2]()
        b3.wait_recv()
        b4.start()
        a3.wait_recv()
        a4.start()
        fillers[3]()
        b4.wait_recv()
        a4.wait_recv()

    def updated(s):
        lt = TILES // nz
        wide = 2 * LANES

        def tile(i):
            top = za_full[s, i // lt, :, i % lt].reshape(ROWS_Z, LANES)
            low = yb_full[s, :, i // lt, i % lt].reshape(ROWS_Y, LANES)
            return jnp.concatenate([top, low], axis=0).astype(F32)

        tail, last = tile(6).T, tile(7).T
        half = LANES // 2
        xs = []
        for m, rest in enumerate((tail[:half], tail[half:], last[:half])):
            main = jnp.concatenate([tile(2 * m), tile(2 * m + 1)], axis=1)
            norm = jnp.sqrt(jnp.sum(main * main, keepdims=True) + jnp.sum(rest * rest, keepdims=True))
            factor = 1.0 / (norm + FROB_EPS)
            main, rest = (main * factor).astype(BF16), (rest * factor).astype(BF16)
            xs.append((main[:wide], main[wide:], rest[:, :wide], rest[:, wide:]))
        for _ in range(NS_STEPS):
            squares = [
                (
                    (dot_nt(p, p) + dot_tn(u, u)).astype(BF16),
                    (dot_nt(q, p) + dot_tn(v, u)).astype(BF16),
                    (dot_nt(q, q) + dot_tn(v, v)).astype(BF16),
                )
                for p, q, u, v in xs
            ]
            mixings = [
                tuple(
                    (NEWTON_B * one.astype(F32) + NEWTON_C * two).astype(BF16)
                    for one, two in (
                        (a, dot(a, a) + dot_tn(b, b)),
                        (b, dot(b, a) + dot(c, b)),
                        (c, dot_nt(b, b) + dot(c, c)),
                    )
                )
                for a, b, c in squares
            ]
            xs = [
                tuple(
                    (NEWTON_A * one.astype(F32) + two).astype(BF16)
                    for one, two in (
                        (p, dot(a, p) + dot_tn(b, q)),
                        (q, dot(b, p) + dot(c, q)),
                        (u, dot(u, a) + dot(v, b)),
                        (v, dot_nt(u, b) + dot(v, c)),
                    )
                )
                for (p, q, u, v), (a, b, c) in zip(xs, mixings)
            ]
        step = step_ref[0]
        for m, (p, q, u, v) in enumerate(xs):
            rest = jnp.concatenate([u, v], axis=1).astype(F32).T
            for rows_at, lanes_at, x in (
                (slice(0, wide), slice(0, wide), p.astype(F32)),
                (slice(wide, dh), slice(0, wide), q.astype(F32)),
                (slice(0, dh), slice(wide, dh), rest),
            ):
                old = w_ref[m, rows_at, lanes_at].astype(F32)
                w_ref[m, rows_at, lanes_at] = (old - step * x).astype(BF16)
        return [w_ref[m] for m in range(3)]

    def applied(s, weights):
        queries = queries_ref[s]
        gate = dot_tn(weights[0], queries)
        up = dot_tn(weights[1], queries)
        hidden = (gate * jax.nn.sigmoid(gate) * up).astype(BF16)
        return dot_tn(hidden, weights[2]).astype(BF16)

    def attend(s):
        first = tok == 0
        scale = 1.0 / math.sqrt(dh)
        queries = queries_ref[s]
        past = dot_tn(queries, halo_ref[s, 0]) * scale
        here = dot_tn(queries, keys_ref[s]) * scale
        row = lax.broadcasted_iota(jnp.int32, (rows, rows), 0)
        col = lax.broadcasted_iota(jnp.int32, (rows, rows), 1)
        limit = jnp.where(first & (s == 0), rows, 0)
        past = jnp.where(col > row + limit, past, -1e30)
        here = jnp.where(col <= row, here, -1e30)
        top = jnp.maximum(
            jnp.max(past, axis=1, keepdims=True), jnp.max(here, axis=1, keepdims=True)
        )
        past = jnp.exp(past - top)
        here = jnp.exp(here - top)
        total = jnp.sum(past, axis=1, keepdims=True) + jnp.sum(here, axis=1, keepdims=True)
        past = (past / total).astype(BF16)
        here = (here / total).astype(BF16)
        return (dot_nt(past, halo_ref[s, 1]) + dot_nt(here, values_ref[s])).astype(BF16)

    piece = dh // PIECES

    def halo(i):
        seg, which, part = i // (2 * PIECES), i // PIECES % 2, pl.ds(i % PIECES * piece, piece)
        ref = (keys_ref, values_ref)[which]
        return remote(
            ref.at[seg, part],
            halo_ref.at[seg, which, part],
            halo_s.at[i],
            halo_r.at[i],
            {"tok": after},
        )

    halos = [halo(i) for i in range(SEGMENTS * 2 * PIECES)]
    halo_at = [0]

    def send_halo(number):
        for copy in halos[halo_at[0] : halo_at[0] + number]:
            copy.start()
        halo_at[0] += number

    def to_heads(send, recv, sems):
        return Exchange(nh, head, lambda p: send.at[p], lambda p: recv.at[p], sems, at_head)

    share_fast = to_heads(fast_send, fast_recv, (fast_s, fast_r))
    share_near = to_heads(near_send, near_recv, (near_s, near_r))
    share_late = to_heads(late_send, late_recv, (late_s, late_r))

    def load(i, src, dst):
        return pltpu.make_async_copy(src, dst, load_s.at[i])

    loads = [
        load(0, k_ref.at[0], keys_ref.at[0]),
        load(1, gate_ref, w_ref.at[0]),
        load(2, up_ref, w_ref.at[1]),
        load(3, v_ref.at[0], values_ref.at[0]),
        load(4, down_ref, w_ref.at[2]),
        load(5, k_ref.at[1], keys_ref.at[1]),
        load(6, v_ref.at[1], values_ref.at[1]),
        load(7, q_ref, queries_ref),
    ]
    for copy in loads:
        copy.start()
    for copy in loads[:5]:
        copy.wait()
    weights = [w_ref[i] for i in range(3)]
    gradients(0, weights)
    for copy in loads[5:]:
        copy.wait()
    pl.semaphore_wait(barrier, (nz - 1) + (ny - 1) + (nh - 1) + 2)

    exchange = plan(0)
    sum_and_share(0, exchange, [lambda n=n: send_halo(n) for n in HALO_AT[:4]])
    send_halo(HALO_AT[4])
    weights = updated(0)
    gradients(1, weights)
    exchange_1 = plan(1)

    def fill_0():
        send_halo(HALO_AT[5])
        fast_send[...] = applied(0, weights).reshape(nh, own, dh)
        share_fast.start()
        fast_recv[head] = fast_send[head]

    def fill_3():
        for copy in halos:
            copy.wait_recv()

        @pl.when(tok == 0)
        def _():
            halo_ref[1] = halo_ref[0]

        for s in range(SEGMENTS):
            near_send[:, s] = attend(s).reshape(nh, own, dh)
        share_near.start()
        near_recv[head] = near_send[head]

    sum_and_share(1, exchange_1, [fill_0, lambda: None, lambda: None, fill_3])
    weights = updated(1)
    late_send[...] = applied(1, weights).reshape(nh, own, dh)
    share_late.start()
    late_recv[head] = late_send[head]

    def scale_of(load):
        total = jnp.zeros((own, dh), F32)
        for p in range(nh):
            wide = load(p).astype(F32)
            total = total + wide * wide
        mean = jnp.sum(total, axis=1, keepdims=True) * (1.0 / (nh * dh))
        return lax.rsqrt(mean + NORM_EPS)

    def scaled(load, gain):
        by = scale_of(load)
        for p in range(0, nh, 2):
            both = jnp.concatenate([load(p), load(p + 1)], axis=1).astype(F32)
            part = slice(p * dh, (p + 2) * dh)
            yield part, both * by * gain_ref[gain : gain + 1, part]

    share_fast.wait_recv()
    for part, value in scaled(lambda p: fast_recv[p], 0):
        out_ref[0, 0, :, part] = value
    share_near.wait_recv()
    for part, value in scaled(lambda p: near_recv[p, 0], 1):
        out_ref[0, 0, :, part] += value
    for part, value in scaled(lambda p: near_recv[p, 1], 1):
        out_ref[1, 0, :, part] = value
    share_late.wait_recv()
    for part, value in scaled(lambda p: late_recv[p], 0):
        out_ref[1, 0, :, part] += value

    for ex in (*exchange, *exchange_1, share_fast, share_near, share_late):
        ex.wait_send()
    for copy in halos:
        copy.wait_send()


def on_device(
    nz,
    ny,
    query_rows,
    key_rows,
    value_rows,
    token_rates,
    gate_weight,
    up_weight,
    down_weight,
    step_size,
    branch_gains,
):
    segments, rows, dh = query_rows.shape
    nh = lax.axis_size("head")
    own = rows // nh
    lt = TILES // nz
    na, nb = ROWS_Z // ny, ROWS_Y // ny
    vmem = pl.BlockSpec(memory_space=pltpu.VMEM)
    hbm = pl.BlockSpec(memory_space=pltpu.HBM)
    S = segments

    def buf(*shape, dtype=BF16):
        return pltpu.VMEM(shape, dtype)

    def pair(*shape):
        return [pltpu.SemaphoreType.DMA(shape), pltpu.SemaphoreType.DMA(shape)]

    return pl.pallas_call(
        functools.partial(kernel, nz, ny, nh),
        out_shape=jax.ShapeDtypeStruct((segments, 1, own, nh * dh), F32),
        in_specs=[hbm] * 3 + [vmem] + [hbm] * 3 + [pl.BlockSpec(memory_space=pltpu.SMEM), vmem],
        out_specs=vmem,
        scratch_shapes=[
            buf(S, nz, ny, lt, na, LANES),
            buf(S, nz, ny, lt, na, LANES),
            buf(S, ny, lt, na, LANES),
            buf(S, ny, lt, na, LANES),
            buf(S, nz, ny, lt, na, LANES),
            buf(S, ny, nz, lt, nb, LANES),
            buf(S, ny, nz, lt, nb, LANES),
            buf(S, nz, lt, nb, LANES),
            buf(S, nz, lt, nb, LANES),
            buf(S, ny, nz, lt, nb, LANES),
            buf(3, dh, dh),
            buf(S, 2, dh, rows),
            buf(S, dh, rows),
            buf(S, dh, rows),
            buf(S, dh, rows),
            buf(nh, own, dh),
            buf(nh, own, dh),
            buf(nh, S, own, dh),
            buf(nh, S, own, dh),
            buf(nh, own, dh),
            buf(nh, own, dh),
            *pair(S, nz),
            *pair(S, ny),
            *pair(S, ny),
            *pair(S, nz),
            *pair(S, ny),
            *pair(S, nz),
            *pair(S, nz),
            *pair(S, ny),
            *pair(S * 2 * PIECES),
            *pair(nh),
            *pair(nh),
            *pair(nh),
            pltpu.SemaphoreType.DMA((8,)),
        ],
        compiler_params=pltpu.CompilerParams(
            collective_id=0, has_side_effects=True, vmem_limit_bytes=67043328
        ),
    )(
        query_rows.swapaxes(1, 2),
        key_rows.swapaxes(1, 2),
        value_rows.swapaxes(1, 2),
        token_rates,
        gate_weight[0],
        up_weight[0],
        down_weight[0],
        step_size,
        branch_gains,
    )


def solution(mesh):
    tok = mesh.shape["tok"]
    ny = 4 if tok >= 32 else 2
    placed = (
        P(None, "tok", "head"),
        P(None, "tok", "head"),
        P(None, "tok", "head"),
        P(None, "head", "tok"),
        P("head", None, None),
        P("head", None, None),
        P("head", None, None),
        P("head"),
        P(),
    )
    return jax.shard_map(
        functools.partial(on_device, tok // ny, ny),
        mesh=mesh,
        in_specs=placed,
        out_specs=P(None, "tok", "head", None),
        check_vma=False,
    )
```

```python
import functools
import math

import jax
import jax.numpy as jnp
from jax import lax
from jax.experimental import pallas as pl
from jax.experimental.pallas import tpu as pltpu
from jax.sharding import PartitionSpec as P

SEGMENTS = 2
WINDOW = 256
NS_STEPS = 3
D = 5120

NEWTON_A = 3.4445
NEWTON_B = -4.775
NEWTON_C = 2.0315
NORM_EPS = 1e-06
FROB_EPS = 1e-07

MESH = pl.DeviceIdType.MESH
BF16 = jnp.bfloat16
F32 = jnp.float32
LANES = 128
ROWS_Z = 160
ROWS_Y = 160
TILES = 8
PIECES = 4
HALO_AT = (2, 2, 2, 0, 4, 2, 2, 2)


def dot(left, right):
    return jnp.dot(left, right, preferred_element_type=F32)


def dot_tn(left, right):
    return lax.dot_general(left, right, (((0,), (0,)), ((), ())), preferred_element_type=F32)


def dot_nt(left, right):
    return lax.dot_general(left, right, (((1,), (1,)), ((), ())), preferred_element_type=F32)


def remote(src, dst, send_sem, recv_sem, where):
    return pltpu.make_async_remote_copy(
        src_ref=src,
        dst_ref=dst,
        send_sem=send_sem,
        recv_sem=recv_sem,
        device_id=where,
        device_id_type=MESH,
    )


class Exchange:
    def __init__(self, count, me, source, slot, sems, where):
        self.count, self.me = count, me
        self.source, self.slot, self.where = source, slot, where
        self.send, self.recv = sems

    def start(self):
        def step(d, _):
            peer = lax.rem(self.me + d, self.count)
            remote(
                self.source(peer),
                self.slot(self.me),
                self.send.at[d],
                self.recv.at[self.me],
                self.where(peer),
            ).start()
            return 0

        lax.fori_loop(1, self.count, step, 0)

    def wait_recv(self):
        def step(d, _):
            peer = lax.rem(self.me + d, self.count)
            remote(
                self.slot(peer), self.slot(peer), self.send.at[d], self.recv.at[peer], self.where(peer)
            ).wait_recv()
            return 0

        lax.fori_loop(1, self.count, step, 0)

    def wait_send(self):
        def step(d, _):
            peer = lax.rem(self.me + d, self.count)
            remote(
                self.source(peer),
                self.slot(self.me),
                self.send.at[d],
                self.recv.at[self.me],
                self.where(peer),
            ).wait_send()
            return 0

        lax.fori_loop(1, self.count, step, 0)


def kernel(
    nz,
    ny,
    nh,
    q_ref,
    k_ref,
    v_ref,
    rate_ref,
    gate_ref,
    up_ref,
    down_ref,
    step_ref,
    gain_ref,
    out_ref,
    za_send,
    za_recv,
    za_part,
    za_recv2,
    za_full,
    yb_send,
    yb_recv,
    yb_part,
    yb_recv2,
    yb_full,
    w_ref,
    halo_ref,
    queries_ref,
    keys_ref,
    values_ref,
    fast_send,
    fast_recv,
    near_send,
    near_recv,
    late_send,
    late_recv,
    *sems,
):
    (za1, zb1, za2, zb2, za3, zb3, za4, zb4) = [(sems[2 * i], sems[2 * i + 1]) for i in range(8)]
    halo_s, halo_r, fast_s, fast_r, near_s, near_r, late_s, late_r, load_s = sems[16:]
    head = lax.axis_index("head")
    tok = lax.axis_index("tok")
    count = nz * ny
    z, y = tok // ny, lax.rem(tok, ny)
    after = lax.rem(tok + 1, count)
    before = lax.rem(tok + count - 1, count)
    dh = q_ref.shape[1]
    rows = q_ref.shape[2]
    own = rows // nh

    def at_z(peer):
        return {"tok": peer * ny + y}

    def at_y(peer):
        return {"tok": z * ny + peer}

    def at_head(peer):
        return {"head": peer}

    barrier = pltpu.get_barrier_semaphore()

    def greet(number, me, where):
        def step(d, _):
            pl.semaphore_signal(
                barrier, inc=1, device_id=where(lax.rem(me + d, number)), device_id_type=MESH
            )
            return 0

        lax.fori_loop(1, number, step, 0)

    greet(nz, z, at_z)
    greet(ny, y, at_y)
    greet(nh, head, at_head)
    pl.semaphore_signal(barrier, inc=1, device_id={"tok": after}, device_id_type=MESH)
    pl.semaphore_signal(barrier, inc=1, device_id={"tok": before}, device_id_type=MESH)

    def gradients(s, weights):
        keys = keys_ref[s]
        pre_gate = dot_tn(weights[0], keys)
        pre_up = dot_tn(weights[1], keys)
        target = (-(rate_ref[s] * values_ref[s].astype(F32))).astype(BF16)
        back = dot(weights[2], target)
        sig = jax.nn.sigmoid(pre_gate)
        swish = pre_gate * sig
        hidden = (swish * pre_up).astype(BF16)
        d_gate = (back * pre_up * sig * (1.0 + pre_gate * (1.0 - sig))).astype(BF16)
        d_up = (back * swish).astype(BF16)
        gg = dot_nt(keys, d_gate)
        gu = dot_nt(keys, d_up)
        gd = dot_nt(hidden, target)
        tiles = [m[:, c : c + LANES] for m in (gg, gu, gd) for c in (0, LANES)]
        tiles.append(jnp.concatenate([gg[:, 256:], gu[:, 256:]], axis=1))
        tiles.append(jnp.concatenate([gd[:, 256:], jnp.zeros_like(gd[:, 256:])], axis=1))
        lt = TILES // nz
        for i, tile in enumerate(tiles):
            for j in range(ny):
                n = ROWS_Z // ny
                za_send[s, i // lt, j, i % lt] = tile[j * n : (j + 1) * n].astype(BF16)
                n = ROWS_Y // ny
                part = tile[ROWS_Z + j * n : ROWS_Z + (j + 1) * n]
                yb_send[s, j, i // lt, i % lt] = part.astype(BF16)

    def plan(s):
        return (
            Exchange(
                nz, z, lambda p: za_send.at[s, p], lambda p: za_recv.at[s, p],
                (za1[0].at[s], za1[1].at[s]), at_z,
            ),
            Exchange(
                ny, y, lambda p: yb_send.at[s, p], lambda p: yb_recv.at[s, p],
                (zb1[0].at[s], zb1[1].at[s]), at_y,
            ),
            Exchange(
                ny, y, lambda p: za_part.at[s, p], lambda p: za_recv2.at[s, p],
                (za2[0].at[s], za2[1].at[s]), at_y,
            ),
            Exchange(
                nz, z, lambda p: yb_part.at[s, p], lambda p: yb_recv2.at[s, p],
                (zb2[0].at[s], zb2[1].at[s]), at_z,
            ),
            Exchange(
                ny, y, lambda p: za_full.at[s, z, y], lambda p: za_full.at[s, z, p],
                (za3[0].at[s], za3[1].at[s]), at_y,
            ),
            Exchange(
                nz, z, lambda p: yb_full.at[s, y, z], lambda p: yb_full.at[s, y, p],
                (zb3[0].at[s], zb3[1].at[s]), at_z,
            ),
            Exchange(
                nz, z, lambda p: za_full.at[s, z], lambda p: za_full.at[s, p],
                (za4[0].at[s], za4[1].at[s]), at_z,
            ),
            Exchange(
                ny, y, lambda p: yb_full.at[s, y], lambda p: yb_full.at[s, p],
                (zb4[0].at[s], zb4[1].at[s]), at_y,
            ),
        )

    def summed(number, me, mine, slots):
        def step(d, total):
            return total + slots(lax.rem(me + d, number)).astype(F32)

        return lax.fori_loop(1, number, step, mine.astype(F32), unroll=True)

    def sum_and_share(s, ex, fillers):
        a1, b1, a2, b2, a3, b3, a4, b4 = ex
        b1.start()
        a1.start()
        fillers[0]()
        b1.wait_recv()
        yb_part[s] = summed(ny, y, yb_send[s, y], lambda p: yb_recv[s, p]).astype(BF16)
        b2.start()
        a1.wait_recv()
        za_part[s] = summed(nz, z, za_send[s, z], lambda p: za_recv[s, p]).astype(BF16)
        a2.start()
        fillers[1]()
        b2.wait_recv()
        yb_full[s, y, z] = summed(nz, z, yb_part[s, z], lambda p: yb_recv2[s, p]).astype(BF16)
        b3.start()
        a2.wait_recv()
        za_full[s, z, y] = summed(ny, y, za_part[s, y], lambda p: za_recv2[s, p]).astype(BF16)
        a3.start()
        fillers[2]()
        b3.wait_recv()
        b4.start()
        a3.wait_recv()
        a4.start()
        fillers[3]()
        b4.wait_recv()
        a4.wait_recv()

    def updated(s):
        lt = TILES // nz
        wide = 2 * LANES

        def tile(i):
            top = za_full[s, i // lt, :, i % lt].reshape(ROWS_Z, LANES)
            low = yb_full[s, :, i // lt, i % lt].reshape(ROWS_Y, LANES)
            return jnp.concatenate([top, low], axis=0).astype(F32)

        tail, last = tile(6).T, tile(7).T
        half = LANES // 2
        xs = []
        for m, rest in enumerate((tail[:half], tail[half:], last[:half])):
            main = jnp.concatenate([tile(2 * m), tile(2 * m + 1)], axis=1)
            norm = jnp.sqrt(jnp.sum(main * main, keepdims=True) + jnp.sum(rest * rest, keepdims=True))
            factor = 1.0 / (norm + FROB_EPS)
            main, rest = (main * factor).astype(BF16), (rest * factor).astype(BF16)
            xs.append((main[:wide], main[wide:], rest[:, :wide], rest[:, wide:]))
        for _ in range(NS_STEPS):
            squares = [
                (
                    (dot_nt(p, p) + dot_tn(u, u)).astype(BF16),
                    (dot_nt(q, p) + dot_tn(v, u)).astype(BF16),
                    (dot_nt(q, q) + dot_tn(v, v)).astype(BF16),
                )
                for p, q, u, v in xs
            ]
            mixings = [
                tuple(
                    (NEWTON_B * one.astype(F32) + NEWTON_C * two).astype(BF16)
                    for one, two in (
                        (a, dot(a, a) + dot_tn(b, b)),
                        (b, dot(b, a) + dot(c, b)),
                        (c, dot_nt(b, b) + dot(c, c)),
                    )
                )
                for a, b, c in squares
            ]
            xs = [
                tuple(
                    (NEWTON_A * one.astype(F32) + two).astype(BF16)
                    for one, two in (
                        (p, dot(a, p) + dot_tn(b, q)),
                        (q, dot(b, p) + dot(c, q)),
                        (u, dot(u, a) + dot(v, b)),
                        (v, dot_nt(u, b) + dot(v, c)),
                    )
                )
                for (p, q, u, v), (a, b, c) in zip(xs, mixings)
            ]
        step = step_ref[0]
        for m, (p, q, u, v) in enumerate(xs):
            rest = jnp.concatenate([u, v], axis=1).astype(F32).T
            for rows_at, lanes_at, x in (
                (slice(0, wide), slice(0, wide), p.astype(F32)),
                (slice(wide, dh), slice(0, wide), q.astype(F32)),
                (slice(0, dh), slice(wide, dh), rest),
            ):
                old = w_ref[m, rows_at, lanes_at].astype(F32)
                w_ref[m, rows_at, lanes_at] = (old - step * x).astype(BF16)
        return [w_ref[m] for m in range(3)]

    def applied(s, weights):
        queries = queries_ref[s]
        gate = dot_tn(weights[0], queries)
        up = dot_tn(weights[1], queries)
        hidden = (gate * jax.nn.sigmoid(gate) * up).astype(BF16)
        return dot_tn(hidden, weights[2]).astype(BF16)

    def attend(s):
        first = tok == 0
        scale = 1.0 / math.sqrt(dh)
        queries = queries_ref[s]
        past = dot_tn(queries, halo_ref[s, 0]) * scale
        here = dot_tn(queries, keys_ref[s]) * scale
        row = lax.broadcasted_iota(jnp.int32, (rows, rows), 0)
        col = lax.broadcasted_iota(jnp.int32, (rows, rows), 1)
        limit = jnp.where(first & (s == 0), rows, 0)
        past = jnp.where(col > row + limit, past, -1e30)
        here = jnp.where(col <= row, here, -1e30)
        top = jnp.maximum(
            jnp.max(past, axis=1, keepdims=True), jnp.max(here, axis=1, keepdims=True)
        )
        past = jnp.exp(past - top)
        here = jnp.exp(here - top)
        total = jnp.sum(past, axis=1, keepdims=True) + jnp.sum(here, axis=1, keepdims=True)
        past = (past / total).astype(BF16)
        here = (here / total).astype(BF16)
        return (dot_nt(past, halo_ref[s, 1]) + dot_nt(here, values_ref[s])).astype(BF16)

    piece = dh // PIECES

    def halo(i):
        seg, which, part = i // (2 * PIECES), i // PIECES % 2, pl.ds(i % PIECES * piece, piece)
        ref = (keys_ref, values_ref)[which]
        return remote(
            ref.at[seg, part],
            halo_ref.at[seg, which, part],
            halo_s.at[i],
            halo_r.at[i],
            {"tok": after},
        )

    halos = [halo(i) for i in range(SEGMENTS * 2 * PIECES)]
    halo_at = [0]

    def send_halo(number):
        for copy in halos[halo_at[0] : halo_at[0] + number]:
            copy.start()
        halo_at[0] += number

    def to_heads(send, recv, sems):
        return Exchange(nh, head, lambda p: send.at[p], lambda p: recv.at[p], sems, at_head)

    share_fast = to_heads(fast_send, fast_recv, (fast_s, fast_r))
    share_near = to_heads(near_send, near_recv, (near_s, near_r))
    share_late = to_heads(late_send, late_recv, (late_s, late_r))

    def load(i, src, dst):
        return pltpu.make_async_copy(src, dst, load_s.at[i])

    loads = [
        load(0, k_ref.at[0], keys_ref.at[0]),
        load(1, gate_ref, w_ref.at[0]),
        load(2, up_ref, w_ref.at[1]),
        load(3, v_ref.at[0], values_ref.at[0]),
        load(4, down_ref, w_ref.at[2]),
        load(5, k_ref.at[1], keys_ref.at[1]),
        load(6, v_ref.at[1], values_ref.at[1]),
        load(7, q_ref, queries_ref),
    ]
    for copy in loads:
        copy.start()
    for copy in loads[:5]:
        copy.wait()
    weights = [w_ref[i] for i in range(3)]
    gradients(0, weights)
    for copy in loads[5:]:
        copy.wait()
    pl.semaphore_wait(barrier, (nz - 1) + (ny - 1) + (nh - 1) + 2)

    exchange = plan(0)
    sum_and_share(0, exchange, [lambda n=n: send_halo(n) for n in HALO_AT[:4]])
    send_halo(HALO_AT[4])
    weights = updated(0)
    gradients(1, weights)
    exchange_1 = plan(1)

    def fill_0():
        send_halo(HALO_AT[5])
        fast_send[...] = applied(0, weights).reshape(nh, own, dh)
        share_fast.start()
        fast_recv[head] = fast_send[head]

    def fill_3():
        for copy in halos:
            copy.wait_recv()

        @pl.when(tok == 0)
        def _():
            halo_ref[1] = halo_ref[0]

        for s in range(SEGMENTS):
            near_send[:, s] = attend(s).reshape(nh, own, dh)
        share_near.start()
        near_recv[head] = near_send[head]

    sum_and_share(1, exchange_1, [fill_0, lambda: send_halo(HALO_AT[6]), lambda: send_halo(HALO_AT[7]), fill_3])
    weights = updated(1)
    late_send[...] = applied(1, weights).reshape(nh, own, dh)
    share_late.start()
    late_recv[head] = late_send[head]

    def scale_of(load):
        total = jnp.zeros((own, dh), F32)
        for p in range(nh):
            wide = load(p).astype(F32)
            total = total + wide * wide
        mean = jnp.sum(total, axis=1, keepdims=True) * (1.0 / (nh * dh))
        return lax.rsqrt(mean + NORM_EPS)

    def scaled(load, gain):
        by = scale_of(load)
        for p in range(0, nh, 2):
            both = jnp.concatenate([load(p), load(p + 1)], axis=1).astype(F32)
            part = slice(p * dh, (p + 2) * dh)
            yield part, both * by * gain_ref[gain : gain + 1, part]

    share_fast.wait_recv()
    for part, value in scaled(lambda p: fast_recv[p], 0):
        out_ref[0, 0, :, part] = value
    share_near.wait_recv()
    for part, value in scaled(lambda p: near_recv[p, 0], 1):
        out_ref[0, 0, :, part] += value
    for part, value in scaled(lambda p: near_recv[p, 1], 1):
        out_ref[1, 0, :, part] = value
    share_late.wait_recv()
    for part, value in scaled(lambda p: late_recv[p], 0):
        out_ref[1, 0, :, part] += value

    for ex in (*exchange, *exchange_1, share_fast, share_near, share_late):
        ex.wait_send()
    for copy in halos:
        copy.wait_send()


def on_device(
    nz,
    ny,
    query_rows,
    key_rows,
    value_rows,
    token_rates,
    gate_weight,
    up_weight,
    down_weight,
    step_size,
    branch_gains,
):
    segments, rows, dh = query_rows.shape
    nh = lax.axis_size("head")
    own = rows // nh
    lt = TILES // nz
    na, nb = ROWS_Z // ny, ROWS_Y // ny
    vmem = pl.BlockSpec(memory_space=pltpu.VMEM)
    hbm = pl.BlockSpec(memory_space=pltpu.HBM)
    S = segments

    def buf(*shape, dtype=BF16):
        return pltpu.VMEM(shape, dtype)

    def pair(*shape):
        return [pltpu.SemaphoreType.DMA(shape), pltpu.SemaphoreType.DMA(shape)]

    return pl.pallas_call(
        functools.partial(kernel, nz, ny, nh),
        out_shape=jax.ShapeDtypeStruct((segments, 1, own, nh * dh), F32),
        in_specs=[hbm] * 3 + [vmem] + [hbm] * 3 + [pl.BlockSpec(memory_space=pltpu.SMEM), vmem],
        out_specs=vmem,
        scratch_shapes=[
            buf(S, nz, ny, lt, na, LANES),
            buf(S, nz, ny, lt, na, LANES),
            buf(S, ny, lt, na, LANES),
            buf(S, ny, lt, na, LANES),
            buf(S, nz, ny, lt, na, LANES),
            buf(S, ny, nz, lt, nb, LANES),
            buf(S, ny, nz, lt, nb, LANES),
            buf(S, nz, lt, nb, LANES),
            buf(S, nz, lt, nb, LANES),
            buf(S, ny, nz, lt, nb, LANES),
            buf(3, dh, dh),
            buf(S, 2, dh, rows),
            buf(S, dh, rows),
            buf(S, dh, rows),
            buf(S, dh, rows),
            buf(nh, own, dh),
            buf(nh, own, dh),
            buf(nh, S, own, dh),
            buf(nh, S, own, dh),
            buf(nh, own, dh),
            buf(nh, own, dh),
            *pair(S, nz),
            *pair(S, ny),
            *pair(S, ny),
            *pair(S, nz),
            *pair(S, ny),
            *pair(S, nz),
            *pair(S, nz),
            *pair(S, ny),
            *pair(S * 2 * PIECES),
            *pair(nh),
            *pair(nh),
            *pair(nh),
            pltpu.SemaphoreType.DMA((8,)),
        ],
        compiler_params=pltpu.CompilerParams(
            collective_id=0, has_side_effects=True, vmem_limit_bytes=67043328
        ),
    )(
        query_rows.swapaxes(1, 2),
        key_rows.swapaxes(1, 2),
        value_rows.swapaxes(1, 2),
        token_rates,
        gate_weight[0],
        up_weight[0],
        down_weight[0],
        step_size,
        branch_gains,
    )


def solution(mesh):
    tok = mesh.shape["tok"]
    ny = 4 if tok >= 32 else 2
    placed = (
        P(None, "tok", "head"),
        P(None, "tok", "head"),
        P(None, "tok", "head"),
        P(None, "head", "tok"),
        P("head", None, None),
        P("head", None, None),
        P("head", None, None),
        P("head"),
        P(),
    )
    return jax.shard_map(
        functools.partial(on_device, tok // ny, ny),
        mesh=mesh,
        in_specs=placed,
        out_specs=P(None, "tok", "head", None),
        check_vma=False,
    )
```
